32 devices in a mesh: fsdp: 4 (over y, core), ctx: 4 (over z), tp: 2 (over x).
Axes of the slice: x: 2, y: 2, z: 4, core: 2. Of those that a mesh axis runs over, the one named last changes fastest.
Arguments:
- tokens: bfloat16 [2, 4, 1056, 1536], P(None, 'fsdp', 'ctx'), may hold values from -6 to 6
- conditioning: bfloat16 [2, 4, 130, 768], P(None, 'fsdp'), may hold values from -6 to 6
- cotangent: bfloat16 [2, 4, 1056, 1536], P(None, 'fsdp', 'ctx'), may hold values from -6 to 6
- live: int32 [2, 4], P(None, 'fsdp'), may hold values from 0 to 1, as said below
- gain_attn: bfloat16 [1536], P('fsdp'), may hold values from 0.5 to 1.5
- w_query: bfloat16 [1536, 1536], P('fsdp', 'tp'), may hold values from -0.15625 to 0.15625
- w_key: bfloat16 [1536, 1536], P('fsdp', 'tp'), may hold values from -0.15625 to 0.15625
- w_value: bfloat16 [1536, 1536], P('fsdp', 'tp'), may hold values from -0.15625 to 0.15625
- w_out: bfloat16 [1536, 1536], P('tp', 'fsdp'), may hold values from -0.625 to 0.625
- gain_cross: bfloat16 [1536], P('fsdp'), may hold values from 0.5 to 1.5
- w_cquery: bfloat16 [1536, 1536], P('fsdp', 'tp'), may hold values from -0.15625 to 0.15625
- w_ckey: bfloat16 [768, 1536], P('fsdp', 'tp'), may hold values from -0.21875 to 0.21875
- w_cvalue: bfloat16 [768, 1536], P('fsdp', 'tp'), may hold values from -0.21875 to 0.21875
- w_cout: bfloat16 [1536, 1536], P('tp', 'fsdp'), may hold values from -0.4375 to 0.4375
- gain_mlp: bfloat16 [1536], P('fsdp'), may hold values from 0.5 to 1.5
- w_gate: bfloat16 [1536, 6144], P('fsdp', 'tp'), may hold values from -0.15625 to 0.15625
- w_up: bfloat16 [1536, 6144], P('fsdp', 'tp'), may hold values from -0.15625 to 0.15625
- w_down: bfloat16 [6144, 1536], P('tp', 'fsdp'), may hold values from -0.078125 to 0.078125
Outputs:
- output: bfloat16 [2, 4, 1056, 1536], P(None, 'fsdp', 'ctx')
- grad_tokens: bfloat16 [2, 4, 1056, 1536], P(None, 'fsdp', 'ctx')
- grad_gain_attn: float32 [1536], P('fsdp')
- grad_query: float32 [1536, 1536], P('fsdp', 'tp')
- grad_key: float32 [1536, 1536], P('fsdp', 'tp')
- grad_value: float32 [1536, 1536], P('fsdp', 'tp')
- grad_out: float32 [1536, 1536], P('tp', 'fsdp')
- grad_gain_cross: float32 [1536], P('fsdp')
- grad_cquery: float32 [1536, 1536], P('fsdp', 'tp')
- grad_ckey: float32 [768, 1536], P('fsdp', 'tp')
- grad_cvalue: float32 [768, 1536], P('fsdp', 'tp')
- grad_cout: float32 [1536, 1536], P('tp', 'fsdp')
- grad_gain_mlp: float32 [1536], P('fsdp')
- grad_gate: float32 [1536, 6144], P('fsdp', 'tp')
- grad_up: float32 [1536, 6144], P('fsdp', 'tp')
- grad_down: float32 [6144, 1536], P('tp', 'fsdp')
The draws below stay inside these ranges and needn't reach their ends.
Inputs may be any that keep to these rules, and one draw needn't show every extreme that they name: Micro-batches before the last have every slot live; the last has exactly 3 live slots.
All inputs are finite; a program needn't handle non-finite values.
Results may differ from the reference program's by a relative error of at most 0.024.
Values may be sent and summed in bfloat16 or wider, within the bound.
A program may use at most 320 MiB of HBM per device.

```python
import jax
import jax.numpy as jnp
from jax import lax

D = 1536
H = 24
HD = 64
FF = 6144
CD = 768
CT = 130
ROT = 32
LEN = 1025
MB = 2
BLK = 264
LENP = 1056
LAST_SEQS = 3
N_FSDP = 4
N_CTX = 4


def draw_live(key, part):
    order = jax.random.permutation(key, N_FSDP)
    last = (order < LAST_SEQS).astype(jnp.int32)
    head = jnp.ones((MB - 1, N_FSDP), jnp.int32)
    return jnp.concatenate([head, last[None, :]], axis=0)


def shard_levels(key, extent, pieces, low, high):
    gain = 1.0
    for dim, parts in pieces:
        steps = jax.random.uniform(jax.random.fold_in(jax.random.fold_in(key, 6), dim), (parts,), jnp.float32, low / len(pieces), high / len(pieces))
        gain = gain * jnp.repeat(jnp.exp(steps), extent[dim] // parts).reshape((-1,) + (1,) * (len(extent) - 1 - dim))
    return gain


def scatter_about(own_key, dims, spread, limit, pieces=(), kind=jnp.bfloat16):
    array = spread * jax.random.normal(own_key, dims, jnp.float32)
    if pieces:
        array = array * shard_levels(own_key, dims, pieces, -0.22, 0.18)
    return jnp.clip(array, -limit, limit).astype(kind)


def setup_inputs(seed: int = 0) -> dict:
    arg_keys = jax.random.split(jax.random.key(seed), 19)
    return {
        "tokens": scatter_about(arg_keys[0], (MB, N_FSDP, LENP, D), 1.0, 6.0, ((1, 4), (2, 4))),
        "conditioning": scatter_about(arg_keys[1], (MB, N_FSDP, CT, CD), 1.0, 6.0, ((1, 4),)),
        "cotangent": scatter_about(arg_keys[2], (MB, N_FSDP, LENP, D), 1.0, 6.0, ((1, 4), (2, 4))),
        "live": draw_live(jax.random.fold_in(arg_keys[18], 71), 0),
        "gain_attn": jnp.clip(1.0 + 0.1 * jax.random.normal(arg_keys[4], (D,), jnp.float32), 0.5, 1.5).astype(jnp.bfloat16),
        "w_query": scatter_about(arg_keys[5], (D, D), D ** -0.5, 0.15625, ((0, 4), (1, 2))),
        "w_key": scatter_about(arg_keys[6], (D, D), D ** -0.5, 0.15625, ((0, 4), (1, 2))),
        "w_value": scatter_about(arg_keys[7], (D, D), D ** -0.5, 0.15625, ((0, 4), (1, 2))),
        "w_out": scatter_about(arg_keys[8], (D, D), (D // 16) ** -0.5, 0.625, ((0, 2), (1, 4))),
        "gain_cross": jnp.clip(1.0 + 0.1 * jax.random.normal(arg_keys[9], (D,), jnp.float32), 0.5, 1.5).astype(jnp.bfloat16),
        "w_cquery": scatter_about(arg_keys[10], (D, D), D ** -0.5, 0.15625, ((0, 4), (1, 2))),
        "w_ckey": scatter_about(arg_keys[11], (CD, D), CD ** -0.5, 0.21875, ((0, 4), (1, 2))),
        "w_cvalue": scatter_about(arg_keys[12], (CD, D), CD ** -0.5, 0.21875, ((0, 4), (1, 2))),
        "w_cout": scatter_about(arg_keys[13], (D, D), (D // 8) ** -0.5, 0.4375, ((0, 2), (1, 4))),
        "gain_mlp": jnp.clip(1.0 + 0.1 * jax.random.normal(arg_keys[14], (D,), jnp.float32), 0.5, 1.5).astype(jnp.bfloat16),
        "w_gate": scatter_about(arg_keys[15], (D, FF), D ** -0.5, 0.15625, ((0, 4), (1, 2))),
        "w_up": scatter_about(arg_keys[16], (D, FF), D ** -0.5, 0.15625, ((0, 4), (1, 2))),
        "w_down": scatter_about(arg_keys[17], (FF, D), FF ** -0.5, 0.078125, ((0, 2), (1, 4))),
    }


@jax.custom_vjp
def low(v):
    return lax.optimization_barrier(v.astype(jnp.bfloat16)).astype(jnp.float32)

@jax.custom_vjp
def low_back(v):
    return v

def low_keep(v):
    return (low(v), None)

def low_pass(kept, grad):
    return (grad,)

def back_keep(v):
    return (v, None)

def back_low(kept, grad):
    return (low(grad),)
low.defvjp(low_keep, low_pass)
low_back.defvjp(back_keep, back_low)
HIGH = lax.Precision.HIGHEST

def mult(left, right):
    return jnp.dot(left, right, precision=HIGH)

def layer_norm(value, norm_gain_vector):
    feature_average = lax.optimization_barrier(jnp.mean(value, -1, keepdims=True))
    cent = value - feature_average
    var = lax.optimization_barrier(jnp.mean(cent * cent, -1, keepdims=True))
    return cent * lax.rsqrt(var + 1e-05) * norm_gain_vector

def slot_info():
    base = LEN // N_CTX
    extra = LEN % N_CTX
    whole = jnp.arange(N_CTX * BLK, dtype=jnp.int32)
    block = whole // BLK
    inner = whole % BLK
    count = base + (block < extra).astype(jnp.int32)
    start = block * base + jnp.minimum(block, extra)
    return (inner < count, start + inner)

def rotate(value, cosine, sine):
    half = ROT // 2
    first = value[..., :half]
    second = value[..., half:ROT]
    return jnp.concatenate([first * cosine - second * sine, second * cosine + first * sine, value[..., ROT:]], axis=-1)

def attend(query, keys, values, key_ok):
    scores = low_back(jnp.einsum('qhd,khd->hqk', query, keys, precision=HIGH) * HD ** (-0.5))
    if key_ok is not None:
        scores = jnp.where(key_ok[None, None, :], scores, -1e+30)
    top = lax.optimization_barrier(jnp.max(scores, -1, keepdims=True))
    expd = jnp.exp(scores - top)
    probs = low(expd / lax.optimization_barrier(jnp.sum(expd, -1, keepdims=True)))
    return jnp.einsum('hqk,khd->qhd', probs, values, precision=HIGH)

def forward(params, seq, conds, key_ok, cosine, sine):
    g1, wq, wk, wv, wo, g2, wqc, wkc, wvc, woc, g3, wg, wu, wd = params
    rows = seq.shape[0]
    h1 = low(layer_norm(seq, g1))
    query = low(rotate(low_back(mult(h1, wq)).reshape(rows, H, HD), cosine, sine))
    keys = low(rotate(low_back(mult(h1, wk)).reshape(rows, H, HD), cosine, sine))
    values = low(low_back(mult(h1, wv))).reshape(rows, H, HD)
    att = low(low_back(attend(query, keys, values, key_ok).reshape(rows, D)))
    x1 = seq + low_back(mult(att, wo))
    h2 = low(layer_norm(x1, g2))
    cquery = low(low_back(mult(h2, wqc))).reshape(rows, H, HD)
    ckeys = low(mult(conds, wkc)).reshape(CT, H, HD)
    cvalues = low(mult(conds, wvc)).reshape(CT, H, HD)
    catt = low(low_back(attend(cquery, ckeys, cvalues, None).reshape(rows, D)))
    x2 = x1 + low_back(mult(catt, woc))
    h3 = low(layer_norm(x2, g3))
    gate = low_back(mult(h3, wg))
    upper = low_back(mult(h3, wu))
    hidden = low(jax.nn.silu(gate) * upper)
    return x2 + low_back(mult(hidden, wd))

def reference(tokens, conditioning, cotangent, live, gain_attn, w_query, w_key, w_value, w_out, gain_cross, w_cquery, w_ckey, w_cvalue, w_cout, gain_mlp, w_gate, w_up, w_down):
    params = tuple((w.astype(jnp.float32) for w in (gain_attn, w_query, w_key, w_value, w_out, gain_cross, w_cquery, w_ckey, w_cvalue, w_cout, gain_mlp, w_gate, w_up, w_down)))
    key_ok, position = slot_info()
    half = ROT // 2
    freq = 10000.0 ** (-jnp.arange(half, dtype=jnp.float32) * 2.0 / ROT)
    angle = position.astype(jnp.float32)[:, None] * freq[None, :]
    cosine = jnp.cos(angle)[:, None, :]
    sine = jnp.sin(angle)[:, None, :]
    count = MB * N_FSDP
    seqs = tokens.astype(jnp.float32).reshape(count, LENP, D)
    conds = conditioning.astype(jnp.float32).reshape(count, CT, CD)
    grads_in = cotangent.astype(jnp.float32).reshape(count, LENP, D)
    alive = live.reshape(count)

    def one(total, item):
        seq, cond_seq, grad_seq, flag = item
        keep = (key_ok & (flag > 0)).astype(jnp.float32)[:, None]
        out, pull = jax.vjp(lambda p, v: forward(p, v, cond_seq, key_ok, cosine, sine), params, seq)
        grads, grad_seq_in = pull(grad_seq * keep)
        total = jax.tree.map(jnp.add, total, grads)
        return (total, ((out * keep).astype(jnp.bfloat16), (grad_seq_in * keep).astype(jnp.bfloat16)))
    start = tuple((jnp.zeros(w.shape, jnp.float32) for w in params))
    total, (outs, grad_outs) = lax.scan(one, start, (seqs, conds, grads_in, alive))
    output = outs.reshape(MB, N_FSDP, LENP, D)
    grad_tokens = grad_outs.reshape(MB, N_FSDP, LENP, D)
    return (output, grad_tokens, total[0], total[1], total[2], total[3], total[4], total[5], total[6], total[7], total[8], total[9], total[10], total[11], total[12], total[13])
```

```python
import functools

import jax
import jax.numpy as jnp
import numpy as np
from jax import lax
from jax.experimental import pallas as pl
from jax.experimental.pallas import tpu as pltpu
from jax.sharding import PartitionSpec as P

HD = 64
ROT = 32
LEN = 1025
F32 = jnp.float32
B16 = jnp.bfloat16
EPS = 1e-05
VMEM_LIMIT = 60 * 1024 * 1024

NN = (((1,), (0,)), ((), ()))
NT = (((1,), (1,)), ((), ()))
TN = (((0,), (0,)), ((), ()))


def dot(a, b, dims=NN):
    return lax.dot_general(a, b, dims, preferred_element_type=F32)


def call(kernel, name, grid, in_specs, out_specs, out_shape, scratch=(), flops=0, bytes_accessed=0, trans=0):
    return pl.pallas_call(
        kernel,
        grid=grid,
        in_specs=in_specs,
        out_specs=out_specs,
        out_shape=out_shape,
        scratch_shapes=list(scratch),
        name=name,
        compiler_params=pltpu.CompilerParams(
            dimension_semantics=("arbitrary",) * len(grid), vmem_limit_bytes=VMEM_LIMIT
        ),
        cost_estimate=pl.CostEstimate(
            flops=int(flops), bytes_accessed=int(bytes_accessed), transcendentals=int(trans)
        ),
    )


def whole(shape):
    zeros = (0,) * len(shape)
    return pl.BlockSpec(shape, lambda *_: zeros)


def shape(dims, kind=B16):
    return jax.ShapeDtypeStruct(dims, kind)


def normalized(v):
    cent = v - jnp.mean(v, -1, keepdims=True)
    inv = lax.rsqrt(jnp.mean(cent * cent, -1, keepdims=True) + EPS)
    return cent * inv, inv


def norm_back(dn, hat, inv, gain):
    dxh = dn * gain
    grad = inv * (
        dxh - jnp.mean(dxh, -1, keepdims=True) - hat * jnp.mean(dxh * hat, -1, keepdims=True)
    )
    return grad, jnp.sum(dn * hat, 0, keepdims=True)


def turned(v, cos, lo, hi):
    wide = v.shape[-1]
    half = ROT // 2
    return v * cos + pltpu.roll(v, wide - half, 1) * lo + pltpu.roll(v, half, 1) * hi


def qkv_kernel(tiles, x_ref, g_ref, w_ref, cos_ref, lo_ref, hi_ref, h_out, q_out, kv_out, h_s):
    j = pl.program_id(0)

    @pl.when(j == 0)
    def _():
        hat, _ = normalized(x_ref[...].astype(F32))
        h = (hat * g_ref[...]).astype(B16)
        h_s[...] = h
        h_out[...] = h

    acc = dot(h_s[...], w_ref[...])

    @pl.when(j < tiles)
    def _():
        q_out[...] = turned(acc, cos_ref[...], lo_ref[...], hi_ref[...]).astype(B16)

    @pl.when(jnp.logical_and(j >= tiles, j < 2 * tiles))
    def _():
        kv_out[...] = turned(acc, cos_ref[...], lo_ref[...], hi_ref[...]).astype(B16)

    @pl.when(j >= 2 * tiles)
    def _():
        kv_out[...] = acc.astype(B16)


def qkv_proj(x, gain, w, tables):
    rows, d = x.shape
    inner = w.shape[1] // 3
    bc = 384
    tiles = inner // bc
    return call(
        functools.partial(qkv_kernel, tiles),
        "qkv_proj",
        (3 * tiles,),
        [
            whole((rows, d)),
            whole((1, d)),
            pl.BlockSpec((d, bc), lambda j: (0, j)),
            whole((rows, bc)),
            whole((rows, bc)),
            whole((rows, bc)),
        ],
        [
            whole((rows, d)),
            pl.BlockSpec((rows, bc), lambda j: (0, jnp.minimum(j, tiles - 1))),
            pl.BlockSpec((rows, bc), lambda j: (0, jnp.maximum(j - tiles, 0))),
        ],
        [shape((rows, d)), shape((rows, inner)), shape((rows, 2 * inner))],
        [pltpu.VMEM((rows, d), B16)],
        2 * rows * d * 3 * inner,
        2 * (2 * rows * d + d * 3 * inner + rows * 3 * inner),
    )(x, gain, w, *tables)


def attn_kernel(n, q_ref, k_ref, v_ref, bias_ref, w_ref, att_out, lse_out, part_out, acc):
    j = pl.program_id(0)
    bias = bias_ref[...]
    outs = []
    lses = []
    for a in range(2):
        lanes = slice(a * HD, (a + 1) * HD)
        qh = q_ref[:, lanes] * jnp.asarray(HD**-0.5, B16)
        s = dot(qh, k_ref[:, lanes], NT) + bias
        top = jnp.max(s, -1, keepdims=True)
        e = jnp.exp(s - top)
        total = jnp.sum(e, -1, keepdims=True)
        outs.append(dot(e.astype(B16), v_ref[:, lanes]) / total)
        lses.append(jnp.broadcast_to(top + jnp.log(total), (s.shape[0], HD)))
    att = jnp.concatenate(outs, 1).astype(B16)
    att_out[...] = att
    lse_out[0] = jnp.concatenate(lses, 1)
    term = dot(att, w_ref[...], NT)

    @pl.when(j == 0)
    def _():
        acc[...] = term

    @pl.when(j > 0)
    def _():
        acc[...] += term

    @pl.when(j == n - 1)
    def _():
        part_out[...] = acc[...].astype(B16)


def attention(q, kv, bias, wo_t):
    rows, inner = q.shape
    keys = kv.shape[0]
    d = wo_t.shape[0]
    n = inner // 128
    return call(
        functools.partial(attn_kernel, n),
        "attention",
        (n,),
        [
            pl.BlockSpec((rows, 128), lambda j: (0, j)),
            pl.BlockSpec((keys, 128), lambda j: (0, j)),
            pl.BlockSpec((keys, 128), lambda j: (0, n + j)),
            whole((1, keys)),
            pl.BlockSpec((d, 128), lambda j: (0, j)),
        ],
        [
            pl.BlockSpec((rows, 128), lambda j: (0, j)),
            pl.BlockSpec((1, rows, 128), lambda j: (j, 0, 0)),
            whole((rows, d)),
        ],
        [shape((rows, inner)), shape((n, rows, 128), F32), shape((rows, d))],
        [pltpu.VMEM((rows, d), F32)],
        4 * rows * keys * inner * 4 + 2 * rows * d * inner,
        2 * (2 * rows * inner + 2 * keys * inner + d * inner + rows * d),
        rows * keys * inner // HD,
    )(q, kv, kv, bias, wo_t)


def cross_kernel(
    n, x_ref, a_ref, b_ref, g_ref, wq_ref, ck_ref, cv_ref, wo_ref,
    x1_out, h_out, cq_out, catt_out, part_out, h_s, acc,
):
    j = pl.program_id(0)

    @pl.when(j == 0)
    def _():
        x1 = x_ref[...].astype(F32) + (a_ref[...].astype(F32) + b_ref[...].astype(F32))
        x1_out[...] = x1
        hat, _ = normalized(x1)
        h = (hat * g_ref[...]).astype(B16)
        h_s[...] = h
        h_out[...] = h

    cq = dot(h_s[...], wq_ref[...]).astype(B16)
    cq_out[...] = cq
    outs = []
    for a in range(cq.shape[1] // HD):
        lanes = slice(a * HD, (a + 1) * HD)
        s = dot(cq[:, lanes] * jnp.asarray(HD**-0.5, B16), ck_ref[:, lanes], NT)
        e = jnp.exp(s - jnp.max(s, -1, keepdims=True))
        total = jnp.sum(e, -1, keepdims=True)
        outs.append(dot(e.astype(B16), cv_ref[:, lanes]) / total)
    catt = jnp.concatenate(outs, 1).astype(B16)
    catt_out[...] = catt
    term = dot(catt, wo_ref[...], NT)

    @pl.when(j == 0)
    def _():
        acc[...] = term

    @pl.when(j > 0)
    def _():
        acc[...] += term

    @pl.when(j == n - 1)
    def _():
        part_out[...] = acc[...].astype(B16)


def cross(x, pa, pb, gain, wcq, ckv, wco_t):
    rows, d = x.shape
    inner = wcq.shape[1]
    cond = ckv.shape[0]
    bc = 256
    n = inner // bc
    col = pl.BlockSpec((rows, bc), lambda j: (0, j))
    return call(
        functools.partial(cross_kernel, n),
        "cross",
        (n,),
        [
            whole((rows, d)),
            whole((rows, d)),
            whole((rows, d)),
            whole((1, d)),
            pl.BlockSpec((d, bc), lambda j: (0, j)),
            pl.BlockSpec((cond, bc), lambda j: (0, j)),
            pl.BlockSpec((cond, bc), lambda j: (0, n + j)),
            pl.BlockSpec((d, bc), lambda j: (0, j)),
        ],
        [whole((rows, d)), whole((rows, d)), col, col, whole((rows, d))],
        [
            shape((rows, d), F32),
            shape((rows, d)),
            shape((rows, inner)),
            shape((rows, inner)),
            shape((rows, d)),
        ],
        [pltpu.VMEM((rows, d), B16), pltpu.VMEM((rows, d), F32)],
        4 * rows * d * inner + 4 * rows * cond * inner * 2,
        2 * (7 * rows * d + 2 * d * inner),
        rows * cond * inner // HD,
    )(x, pa, pb, gain, wcq, ckv, ckv, wco_t)


def mlp_kernel(
    n, micro, *refs
):
    (x1_refs, a_refs, b_refs) = (refs[:micro], refs[micro : 2 * micro], refs[2 * micro : 3 * micro])
    (g_ref, gy_ref, wg_ref, wu_ref, wd_ref, x2_out, h_out, hid_out, dg_out, du_out, y_out, dh_out,
     h_s, y_s, dh_s) = refs[3 * micro :]
    j = pl.program_id(0)
    rows = x1_refs[0].shape[0]

    @pl.when(j == 0)
    def _():
        for m in range(micro):
            part = pl.ds(m * rows, rows)
            x2 = x1_refs[m][...] + (a_refs[m][...].astype(F32) + b_refs[m][...].astype(F32))
            x2_out[part, :] = x2
            hat, _ = normalized(x2)
            h = (hat * g_ref[...]).astype(B16)
            h_s[part, :] = h
            h_out[part, :] = h

    h = h_s[...]
    gate = dot(h, wg_ref[...])
    up = dot(h, wu_ref[...])
    dhid = dot(gy_ref[...], wd_ref[...])
    sig = jax.nn.sigmoid(gate)
    act = gate * sig
    hid = (act * up).astype(B16)
    dg = (dhid * up * sig * (1.0 + gate * (1.0 - sig))).astype(B16)
    du = (dhid * act).astype(B16)
    hid_out[...] = hid
    dg_out[...] = dg
    du_out[...] = du
    y = dot(hid, wd_ref[...], NT)
    dh = dot(dg, wg_ref[...], NT) + dot(du, wu_ref[...], NT)

    @pl.when(j == 0)
    def _():
        y_s[...] = y
        dh_s[...] = dh

    @pl.when(j > 0)
    def _():
        y_s[...] += y
        dh_s[...] += dh

    @pl.when(j == n - 1)
    def _():
        y_out[...] = y_s[...].astype(B16)
        dh_out[...] = dh_s[...].astype(B16)


def mlp(x1s, pas, pbs, gain, gyb, wg, wu, wd_t):
    micro = len(x1s)
    rows, d = x1s[0].shape
    total = micro * rows
    hidden = wg.shape[1]
    bc = 256
    n = hidden // bc
    once = lambda s: pl.BlockSpec(s, lambda j: (0, 0), pipeline_mode=pl.Buffered(1))
    wcol = pl.BlockSpec((d, bc), lambda j: (0, j))
    ocol = pl.BlockSpec((total, bc), lambda j: (0, j))
    return call(
        functools.partial(mlp_kernel, n, micro),
        "mlp",
        (n,),
        [once((rows, d))] * (3 * micro)
        + [whole((1, d)), once((total, d)), wcol, wcol, wcol],
        [once((total, d)), once((total, d)), ocol, ocol, ocol, once((total, d)), once((total, d))],
        [
            shape((total, d), F32),
            shape((total, d)),
            shape((total, hidden)),
            shape((total, hidden)),
            shape((total, hidden)),
            shape((total, d)),
            shape((total, d)),
        ],
        [pltpu.VMEM((total, d), B16), pltpu.VMEM((total, d), F32), pltpu.VMEM((total, d), F32)],
        12 * total * d * hidden,
        2 * (3 * d * hidden + 3 * total * hidden + 10 * total * d),
        total * hidden,
    )(*x1s, *pas, *pbs, gain, gyb, wg, wu, wd_t)


def cross_back_kernel(
    n, x2_ref, gy_ref, a_ref, b_ref, g_ref, cq_ref, ck_ref, cv_ref, wo_ref, wq_ref,
    g2x_out, gc_out, gg_out, dcq_out, dck_out, dcv_out, part_out, gc_s, acc,
):
    j = pl.program_id(0)

    @pl.when(j == 0)
    def _():
        hat, inv = normalized(x2_ref[...])
        dn = a_ref[...].astype(F32) + b_ref[...].astype(F32)
        grad, gg = norm_back(dn, hat, inv, g_ref[...])
        gg_out[...] = gg
        g2x = gy_ref[...].astype(F32) + grad
        g2x_out[...] = g2x
        gc = g2x.astype(B16)
        gc_s[...] = gc
        gc_out[...] = gc

    dca = dot(gc_s[...], wo_ref[...]).astype(B16)
    dqs = []
    dks = []
    dvs = []
    for a in range(dca.shape[1] // HD):
        lanes = slice(a * HD, (a + 1) * HD)
        cqh = cq_ref[:, lanes] * jnp.asarray(HD**-0.5, B16)
        ckh = ck_ref[:, lanes]
        s = dot(cqh, ckh, NT)
        e = jnp.exp(s - jnp.max(s, -1, keepdims=True))
        p = e / jnp.sum(e, -1, keepdims=True)
        dp = dot(dca[:, lanes], cv_ref[:, lanes], NT)
        ds = (p * (dp - jnp.sum(p * dp, -1, keepdims=True))).astype(B16)
        dqs.append(dot(ds, ckh) * HD**-0.5)
        dks.append(dot(ds, cqh, TN))
        dvs.append(dot(p.astype(B16), dca[:, lanes], TN))
    dcq = jnp.concatenate(dqs, 1).astype(B16)
    dcq_out[...] = dcq
    dck_out[...] = jnp.concatenate(dks, 1).astype(B16)
    dcv_out[...] = jnp.concatenate(dvs, 1).astype(B16)
    term = dot(dcq, wq_ref[...], NT)

    @pl.when(j == 0)
    def _():
        acc[...] = term

    @pl.when(j > 0)
    def _():
        acc[...] += term

    @pl.when(j == n - 1)
    def _():
        part_out[...] = acc[...].astype(B16)


def cross_back(m, x2, gyb, pa, pb, gain, cq, ckv, wco_t, wcq):
    rows, inner = cq.shape
    d = x2.shape[1]
    cond = ckv.shape[0]
    bc = 256
    n = inner // bc
    row = pl.BlockSpec((rows, d), lambda j: (m, 0))
    col = pl.BlockSpec((rows, bc), lambda j: (0, j))
    ccol = pl.BlockSpec((cond, bc), lambda j: (0, j))
    wcol = pl.BlockSpec((d, bc), lambda j: (0, j))
    return call(
        functools.partial(cross_back_kernel, n),
        "cross_back",
        (n,),
        [
            row,
            row,
            whole((rows, d)),
            whole((rows, d)),
            whole((1, d)),
            col,
            ccol,
            pl.BlockSpec((cond, bc), lambda j: (0, n + j)),
            wcol,
            wcol,
        ],
        [whole((rows, d)), whole((rows, d)), whole((1, d)), col, ccol, ccol, whole((rows, d))],
        [
            shape((rows, d), F32),
            shape((rows, d)),
            shape((1, d), F32),
            shape((rows, inner)),
            shape((cond, inner)),
            shape((cond, inner)),
            shape((rows, d)),
        ],
        [pltpu.VMEM((rows, d), B16), pltpu.VMEM((rows, d), F32)],
        4 * rows * d * inner + 10 * rows * cond * inner * 2,
        2 * (10 * rows * d + 2 * d * inner),
        rows * cond * inner // HD,
    )(x2, gyb, pa, pb, gain, cq, ckv, ckv, wco_t, wcq)


def attn_back_kernel(
    x1_ref, g2x_ref, a_ref, b_ref, g_ref, wo_ref, q_ref, k_ref, v_ref, lse_ref, bias_ref,
    cos_ref, lo_ref, hi_ref,
    g1x_out, ga_out, gg_out, dq_out, dk_out, dv_out, ga_s,
):
    j = pl.program_id(0)

    @pl.when(j == 0)
    def _():
        hat, inv = normalized(x1_ref[...])
        dn = a_ref[...].astype(F32) + b_ref[...].astype(F32)
        grad, gg = norm_back(dn, hat, inv, g_ref[...])
        gg_out[...] = gg
        g1x = g2x_ref[...] + grad
        g1x_out[...] = g1x
        ga = g1x.astype(B16)
        ga_s[...] = ga
        ga_out[...] = ga

    datt = dot(ga_s[...], wo_ref[...]).astype(B16)
    bias = bias_ref[...]
    dqs = []
    dks = []
    dvs = []
    for a in range(2):
        lanes = slice(a * HD, (a + 1) * HD)
        qh = q_ref[:, lanes] * jnp.asarray(HD**-0.5, B16)
        kh = k_ref[:, lanes]
        s = dot(qh, kh, NT) + bias
        p = jnp.exp(s - lse_ref[0, :, a * HD : a * HD + 1])
        dp = dot(datt[:, lanes], v_ref[:, lanes], NT)
        ds = (p * (dp - jnp.sum(p * dp, -1, keepdims=True))).astype(B16)
        dqs.append(dot(ds, kh) * HD**-0.5)
        dks.append(dot(ds, qh, TN))
        dvs.append(dot(p.astype(B16), datt[:, lanes], TN))
    dq = jnp.concatenate(dqs, 1)
    dq_out[...] = turned(dq, cos_ref[...], -lo_ref[...], -hi_ref[...]).astype(B16)
    dk_out[...] = jnp.concatenate(dks, 1).astype(B16)
    dv_out[...] = jnp.concatenate(dvs, 1).astype(B16)


def attention_back(x1, g2x, pa, pb, gain, wo_t, q, kv, lse, bias, tables):
    rows, inner = q.shape
    d = x1.shape[1]
    keys = kv.shape[0]
    n = inner // 128
    col = pl.BlockSpec((rows, 128), lambda j: (0, j))
    kcol = pl.BlockSpec((keys, 128), lambda j: (0, j))
    return call(
        attn_back_kernel,
        "attention_back",
        (n,),
        [
            whole((rows, d)),
            whole((rows, d)),
            whole((rows, d)),
            whole((rows, d)),
            whole((1, d)),
            pl.BlockSpec((d, 128), lambda j: (0, j)),
            col,
            kcol,
            pl.BlockSpec((keys, 128), lambda j: (0, n + j)),
            pl.BlockSpec((1, rows, 128), lambda j: (j, 0, 0)),
            whole((1, keys)),
            pl.BlockSpec((rows, 128), lambda j: (0, 0)),
            pl.BlockSpec((rows, 128), lambda j: (0, 0)),
            pl.BlockSpec((rows, 128), lambda j: (0, 0)),
        ],
        [whole((rows, d)), whole((rows, d)), whole((1, d)), col, kcol, kcol],
        [
            shape((rows, d), F32),
            shape((rows, d)),
            shape((1, d), F32),
            shape((rows, inner)),
            shape((keys, inner)),
            shape((keys, inner)),
        ],
        [pltpu.VMEM((rows, d), B16)],
        10 * rows * keys * inner * 4 + 2 * rows * d * inner,
        2 * (8 * rows * d + 4 * keys * inner + d * inner),
        rows * keys * inner // HD,
    )(x1, g2x, pa, pb, gain, wo_t, q, kv, kv, lse, bias, *tables)


def qkv_back_kernel(n, tiles, dq_ref, dk_ref, dv_ref, w_ref, cos_ref, lo_ref, hi_ref, all_out, part_out, t_s, acc):
    j = pl.program_id(0)

    @pl.when(j < tiles)
    def _():
        t_s[...] = dq_ref[...]

    @pl.when(jnp.logical_and(j >= tiles, j < 2 * tiles))
    def _():
        t_s[...] = turned(
            dk_ref[...].astype(F32), cos_ref[...], -lo_ref[...], -hi_ref[...]
        ).astype(B16)

    @pl.when(j >= 2 * tiles)
    def _():
        t_s[...] = dv_ref[...]

    all_out[...] = t_s[...]
    term = dot(t_s[...], w_ref[...], NT)

    @pl.when(j == 0)
    def _():
        acc[...] = term

    @pl.when(j > 0)
    def _():
        acc[...] += term

    @pl.when(j == n - 1)
    def _():
        part_out[...] = acc[...].astype(B16)


def qkv_back(dq, dk, dv, w, tables):
    rows, inner = dq.shape
    d = w.shape[0]
    bc = 384
    tiles = inner // bc
    n = 3 * tiles
    last = tiles - 1
    return call(
        functools.partial(qkv_back_kernel, n, tiles),
        "qkv_back",
        (n,),
        [
            pl.BlockSpec((rows, bc), lambda j: (0, jnp.minimum(j, last))),
            pl.BlockSpec((rows, bc), lambda j: (0, jnp.clip(j - tiles, 0, last))),
            pl.BlockSpec((rows, bc), lambda j: (0, jnp.clip(j - 2 * tiles, 0, last))),
            pl.BlockSpec((d, bc), lambda j: (0, j)),
            whole((rows, bc)),
            whole((rows, bc)),
            whole((rows, bc)),
        ],
        [pl.BlockSpec((rows, bc), lambda j: (0, j)), whole((rows, d))],
        [shape((rows, 3 * inner)), shape((rows, d))],
        [pltpu.VMEM((rows, bc), B16), pltpu.VMEM((rows, d), F32)],
        2 * rows * d * 3 * inner,
        2 * (6 * rows * inner + d * 3 * inner + rows * d),
    )(dq, dk, dv, w, *tables)


def input_back_kernel(x_ref, g1x_ref, a_ref, b_ref, g_ref, keep_ref, gx_out, gg_out):
    hat, inv = normalized(x_ref[...].astype(F32))
    dn = a_ref[...].astype(F32) + b_ref[...].astype(F32)
    grad, gg = norm_back(dn, hat, inv, g_ref[...])
    gg_out[...] = gg
    gx_out[...] = ((g1x_ref[...] + grad) * keep_ref[...]).astype(B16)


def input_back(x, g1x, pa, pb, gain, keep):
    rows, d = x.shape
    return call(
        input_back_kernel,
        "input_back",
        (1,),
        [whole((rows, d))] * 4 + [whole((1, d)), whole((rows, 1))],
        [whole((rows, d)), whole((1, d))],
        [shape((rows, d)), shape((1, d), F32)],
        (),
        0,
        14 * rows * d,
    )(x, g1x, pa, pb, gain, keep)


def wgrad_kernel(k, order_ref, *refs):
    out = refs[-1]
    total = dot(refs[0][...], refs[k][...], TN)
    for i in range(1, k):
        total += dot(refs[i][...], refs[k + i][...], TN)
    out[...] = total.astype(B16)


def weight_grad(lefts, rights, order, rb, bc=768):
    k = len(lefts)
    rows, d = lefts[0].shape
    cols = rights[0].shape[1]
    bc = min(bc, cols)
    return pl.pallas_call(
        functools.partial(wgrad_kernel, k),
        grid_spec=pltpu.PrefetchScalarGridSpec(
            num_scalar_prefetch=1,
            grid=(cols // bc, d // rb),
            in_specs=[pl.BlockSpec((rows, rb), lambda j, o, t: (0, t[o]))] * k
            + [pl.BlockSpec((rows, bc), lambda j, o, t: (0, j))] * k,
            out_specs=pl.BlockSpec((rb, bc), lambda j, o, t: (o, j)),
        ),
        out_shape=shape((d, cols)),
        name="weight_grad",
        compiler_params=pltpu.CompilerParams(
            dimension_semantics=("arbitrary", "arbitrary"), vmem_limit_bytes=VMEM_LIMIT
        ),
        cost_estimate=pl.CostEstimate(
            flops=2 * k * rows * d * cols,
            bytes_accessed=2 * (k * rows * (d * (cols // bc) + cols) + d * cols),
            transcendentals=0,
        ),
    )(order, *lefts, *rights)


def swap(v, axis, bit):
    n = lax.axis_size(axis)
    return lax.ppermute(v, axis, [(i, i ^ bit) for i in range(n)])


def scatter_sum(v, n):
    bit = 1
    while bit < n:
        half = v.shape[0] // 2
        v = v[:half] + swap(v[half:], "fsdp", bit)
        bit *= 2
    return v


def xor_order(n):
    order = [0]
    bit = n // 2
    while bit:
        order = order + [o ^ bit for o in order]
        bit //= 2
    return order


def line_sum(v):
    z = lax.axis_index("ctx")
    left = z == 1
    half = v.shape[0] // 2
    v = v + lax.ppermute(v, "ctx", [(0, 1), (3, 2)])
    top, low = v[:half], v[half:]
    got = lax.ppermute(jnp.where(left, low, top), "ctx", [(1, 2), (2, 1)])
    mine = jnp.where(left, top, low) + got
    other = lax.ppermute(mine, "ctx", [(1, 2), (2, 1)])
    full = jnp.concatenate([jnp.where(left, mine, other), jnp.where(left, other, mine)], 0)
    out = lax.ppermute(full, "ctx", [(1, 0), (2, 3)])
    return jnp.where((z == 1) | (z == 2), full, out)


def per_device(
    tokens, conditioning, cotangent, live,
    gain_attn, w_query, w_key, w_value, w_out,
    gain_cross, w_cquery, w_ckey, w_cvalue, w_cout,
    gain_mlp, w_gate, w_up, w_down,
):
    micro = tokens.shape[0]
    blk = tokens.shape[2]
    d = tokens.shape[3]
    rows = -(-blk // 16) * 16
    inner = w_query.shape[1]
    cond_rows = conditioning.shape[2]
    nf = lax.axis_size("fsdp")
    me = lax.axis_index("fsdp")
    ctx_count = lax.axis_size("ctx")
    here = lax.axis_index("ctx")
    base = LEN // ctx_count
    extra = LEN % ctx_count
    first = here * base + jnp.minimum(here, extra)
    own = base + (here < extra).astype(jnp.int32)
    idx = jnp.arange(rows, dtype=jnp.int32)
    row_ok = idx < own
    position = (first + idx).astype(F32)
    slots = np.arange(rows * ctx_count)
    ok = slots % rows < base + (slots // rows < extra)
    bias = jnp.asarray(np.where(ok, 0.0, -1e30).astype(np.float32))[None, :]
    half = ROT // 2
    lane = np.arange(384) % HD
    freq = 10000.0 ** (-np.arange(half, dtype=np.float64) * 2.0 / ROT)
    per_lane = jnp.asarray(np.where(lane < ROT, freq[lane % half], 0.0).astype(np.float32))
    angle = position[:, None] * per_lane[None, :]
    sine = jnp.sin(angle)
    tables = (
        jnp.cos(angle),
        jnp.where(jnp.asarray(lane < half)[None, :], -sine, 0.0),
        jnp.where(jnp.asarray((lane >= half) & (lane < ROT))[None, :], sine, 0.0),
    )

    def gather(w):
        return lax.all_gather(w, "fsdp", axis=0, tiled=True)

    w_qkv = gather(jnp.concatenate([w_query, w_key, w_value], 1))
    gains = gather(jnp.stack([gain_attn, gain_cross, gain_mlp], 1)).astype(F32).T
    wo_t, wcq, wco_t = jnp.split(
        gather(jnp.concatenate([w_out.T, w_cquery, w_cout.T], 1)), 3, axis=1
    )
    w_ckv = gather(jnp.concatenate([w_ckey, w_cvalue], 1))
    wg = gather(w_gate)
    wu = gather(w_up)
    wd_t = gather(w_down.T)
    g1, g2, g3 = gains[0:1], gains[1:2], gains[2:3]

    pad = ((0, 0), (0, rows - blk), (0, 0))
    x_all = jnp.pad(tokens[:, 0], pad)
    xs = [x_all[m] for m in range(micro)]
    keeps = [(row_ok & (live[m, 0] > 0)).astype(F32)[:, None] for m in range(micro)]
    gyb = (
        jnp.pad(cotangent[:, 0], pad).astype(F32) * jnp.stack(keeps)
    ).astype(B16).reshape(micro * rows, d)
    conds = [conditioning[m, 0] for m in range(micro)]

    def tp(v):
        return swap(v, "tp", 1)

    h1s, qs, kvs = [], [], []
    for m in range(micro):
        h1, q, kv = qkv_proj(xs[m], g1, w_qkv, tables)
        h1s.append(h1)
        qs.append(q)
        kvs.append(lax.all_gather(kv, "ctx", axis=0, tiled=True))
    ckvs = [jnp.dot(conds[m], w_ckv, preferred_element_type=F32).astype(B16) for m in range(micro)]
    atts, lses, x1s, h2s, cqs, catts, pas, pbs = [], [], [], [], [], [], [], []
    for m in range(micro):
        att, lse, part = attention(qs[m], kvs[m], bias, wo_t)
        x1, h2, cq, catt, part2 = cross(xs[m], part, tp(part), g2, wcq, ckvs[m], wco_t)
        atts.append(att)
        lses.append(lse)
        x1s.append(x1)
        h2s.append(h2)
        cqs.append(cq)
        catts.append(catt)
        pas.append(part2)
        pbs.append(tp(part2))
    x2, h3, hid, dg, du, y_part, dh_part = mlp(x1s, pas, pbs, g3, gyb, wg, wu, wd_t)
    y_other = tp(y_part)
    result = x2 + (y_part.astype(F32) + y_other.astype(F32))
    output = (result.reshape(micro, rows, d) * jnp.stack(keeps)).astype(B16)[:, None, :blk]

    if (d // nf) % 128 == 0:
        order = (me ^ jnp.asarray(xor_order(nf), jnp.int32)).astype(jnp.int32)
        rb = d // nf
        arranged = lambda h: h
    else:
        rb = 384
        order = jnp.arange(d // rb, dtype=jnp.int32)
        piece = d // nf

        def arranged(h):
            return jnp.concatenate(
                [
                    lax.dynamic_slice_in_dim(h, (me ^ o) * piece, piece, 1)
                    for o in xor_order(nf)
                ],
                1,
            )

    def reduced(lefts, rights):
        g = weight_grad([arranged(h) for h in lefts], rights, order, rb)
        return line_sum(scatter_sum(g, nf)).astype(F32)

    grad_down = reduced([gyb], [hid]).T
    grad_gate = reduced([h3], [dg])
    grad_up = reduced([h3], [du])

    gcs, gg3s, dcqs, dckvs, gas, gg2s, gg1s, dqkvs, gxs = [], [], [], [], [], [], [], [], []
    for m in range(micro):
        dha = dh_part[m * rows : (m + 1) * rows]
        g2x, gc, gg3, dcq, dck, dcv, part3 = cross_back(
            m, x2, gyb, dha, tp(dha), g3, cqs[m], ckvs[m], wco_t, wcq
        )
        g1x, ga, gg2, dq, dk, dv = attention_back(
            x1s[m], g2x, part3, tp(part3), g2, wo_t, qs[m], kvs[m], lses[m], bias, tables
        )
        dkv = lax.psum_scatter(
            jnp.concatenate([dk, dv], 1), "ctx", scatter_dimension=0, tiled=True
        )
        dqkv, part4 = qkv_back(dq, dkv[:, :inner], dkv[:, inner:], w_qkv, tables)
        gx, gg1 = input_back(xs[m], g1x, part4, tp(part4), g1, keeps[m])
        gcs.append(gc)
        gg3s.append(gg3)
        dcqs.append(dcq)
        dckvs.append(jnp.concatenate([dck, dcv], 1))
        gas.append(ga)
        gg2s.append(gg2)
        dqkvs.append(dqkv)
        gg1s.append(gg1)
        gxs.append(gx)
    grad_tokens = jnp.stack(gxs)[:, None, :blk]

    grad_cout = reduced(gcs, catts).T
    grad_cquery = reduced(h2s, dcqs)
    cond_cat = jnp.concatenate(conds, 0)
    cpiece = cond_cat.shape[1] // nf
    cond_cat = jnp.concatenate(
        [lax.dynamic_slice_in_dim(cond_cat, (me ^ o) * cpiece, cpiece, 1) for o in xor_order(nf)], 1
    )
    grad_ckv = jnp.einsum(
        "rc,rk->ck", cond_cat, jnp.concatenate(dckvs, 0), preferred_element_type=F32
    ).astype(B16)
    grad_ckv = line_sum(scatter_sum(grad_ckv, nf)).astype(F32)
    grad_out = reduced(gas, atts).T
    grad_qkv = reduced(h1s, dqkvs)
    gg = jnp.concatenate([sum(gg1s), sum(gg2s), sum(gg3s)], 0)
    gg = lax.psum(gg, ("fsdp", "ctx"))
    gg = lax.dynamic_slice_in_dim(gg, me * (d // nf), d // nf, 1)
    return (
        output,
        grad_tokens,
        gg[0],
        grad_qkv[:, :inner],
        grad_qkv[:, inner : 2 * inner],
        grad_qkv[:, 2 * inner :],
        grad_out,
        gg[1],
        grad_cquery,
        grad_ckv[:, :inner],
        grad_ckv[:, inner:],
        grad_cout,
        gg[2],
        grad_gate,
        grad_up,
        grad_down,
    )


def solution(mesh):
    acts = P(None, "fsdp", "ctx", None)
    rows = P("fsdp", "tp")
    cols = P("tp", "fsdp")
    vec = P("fsdp")
    weights = (vec, rows, rows, rows, cols, vec, rows, rows, rows, cols, vec, rows, rows, cols)
    return jax.shard_map(
        per_device,
        mesh=mesh,
        in_specs=(acts, P(None, "fsdp", None, None), acts, P(None, "fsdp")) + weights,
        out_specs=(acts, acts) + weights,
        check_vma=False,
    )
```
